32 devices in a mesh: blk: 8 (over z, x), team: 4 (over y, core).
Axes of the slice: x: 2, y: 2, z: 4, core: 2. Of those that a mesh axis runs over, the one named last changes fastest.
Arguments:
- points: float32 [2048, 1024], P('blk'), may hold values from -80 to 80
- probes: float32 [2048, 256], P('blk'), may hold values from -6 to 6
Outputs:
- product: float32 [2048, 256], P(('blk', 'team'))
The draws below stay inside these ranges and needn't reach their ends.
All inputs are finite; a program needn't handle non-finite values.
Results may differ from the reference program's by a relative error of at most 0.00014.
Values sent between devices are 32-bit elements; how exact they have to be, the bound alone decides.
A program may use at most 64 MiB of HBM per device.

```python
import jax
import jax.numpy as jnp
from jax import lax

D = 1024
R = 256
LATENT = 16
ROWS = 256
POINTS = 2048
N_BLK = 8


def draw_points(key, part):
    first = jax.random.fold_in(key, 11)
    second = jax.random.fold_in(key, 23)
    third = jax.random.fold_in(key, 37)
    latent = jnp.clip(jax.random.normal(first, (POINTS, LATENT), jnp.float32), -4.0, 4.0)
    mixing = jnp.clip(jax.random.normal(second, (LATENT, D), jnp.float32), -4.0, 4.0) / 4.0
    noise = jnp.clip(jax.random.normal(third, (POINTS, D), jnp.float32), -4.0, 4.0) * 0.3
    return jnp.dot(latent, mixing) + noise


def block_scale(own_key, dims, shards, smallest, high):
    gain, own = 1.0, jax.random.fold_in(own_key, 6)
    for axis_at, parts in shards:
        steps = jnp.exp(jax.random.uniform(jax.random.fold_in(own, axis_at), (parts,), jnp.float32, smallest / len(shards), high / len(shards)))
        gain = gain * jnp.repeat(steps, dims[axis_at] // parts).reshape([-1 if axis == axis_at else 1 for axis in range(len(dims))])
    return gain


def bell_draw(own_key, extent, spread, most, pieces=(), dtype=jnp.bfloat16):
    factor_of = block_scale(own_key, extent, pieces, -0.22, 0.18) if pieces else 1.0
    drawn = jax.random.normal(own_key, extent, jnp.float32) * spread * factor_of
    return jnp.minimum(jnp.maximum(drawn, -most), most).astype(dtype)


def setup_inputs(seed: int = 0) -> dict:
    seeds = jax.random.split(jax.random.key(seed), 3)
    points = draw_points(jax.random.fold_in(seeds[2], 71), 0)
    probes = bell_draw(seeds[1], (POINTS, R), 1.0, 6.0, ((0, 8),), jnp.float32)
    return dict(points=points, probes=probes)


def reference(points, probes):
    scale = 2.0 / points.shape[1]
    sq = jnp.sum(points * points, axis=1)
    blocks = points.reshape(N_BLK, ROWS, points.shape[1])
    sq_blocks = sq.reshape(N_BLK, ROWS)

    def one_block(pair):
        rows, rows_sq = pair
        cross = lax.dot_general(rows, points, (((1,), (1,)), ((), ())), precision=lax.Precision.HIGHEST, preferred_element_type=jnp.float32)
        arg = (rows_sq[:, None] + sq[None, :] - 2.0 * cross) * scale
        kernel = jnp.exp(-jnp.maximum(arg, 0.0))
        return jnp.dot(kernel, probes, precision=lax.Precision.HIGHEST, preferred_element_type=jnp.float32)

    result = lax.map(one_block, (blocks, sq_blocks))
    return result.reshape(N_BLK * ROWS, probes.shape[1])
```

```python
import functools

import jax
import jax.numpy as jnp
from jax import lax
from jax.experimental import pallas as pl
from jax.experimental.pallas import tpu as pltpu
from jax.sharding import PartitionSpec as P

HIGHEST = lax.Precision.HIGHEST
MESH = pl.DeviceIdType.MESH


def kernel(
    blocks,
    outer,
    inner,
    team_size,
    points_hbm,
    probes_hbm,
    out_ref,
    own,
    own_probes,
    all_points,
    all_probes,
    own_sq,
    total,
    parts,
    load_sem,
    recv_sem,
    extra_recv,
    send_outer,
    send_inner,
    extra_send,
    part_send,
    part_recv,
):
    rows, width = own.shape
    piece = rows // team_size
    half = piece // 2
    scale = 2.0 / width
    block = lax.axis_index("blk")
    team = lax.axis_index("team")
    z = block // inner
    x = lax.rem(block, inner)
    split = inner == 2 and outer > 2

    def at(layer, column):
        return layer * inner + column

    def rows_of(index, offset, count):
        return pl.ds(pl.multiple_of(index * piece + offset, half), count)

    def copy_pair(source, where, target, send, recv):
        made = []
        for which, (src, dst) in enumerate(((source[0], all_points), (source[1], all_probes))):
            made.append(
                pltpu.make_async_remote_copy(
                    src_ref=src,
                    dst_ref=dst.at[where],
                    send_sem=send.at[which],
                    recv_sem=recv.at[which],
                    device_id={"blk": target},
                    device_id_type=MESH,
                )
            )
        return made

    def gathered(where):
        return all_points.at[where], all_probes.at[where]

    own_rows = pl.ds(pl.multiple_of(team * piece, piece), piece)
    own_source = points_hbm.at[own_rows], probes_hbm.at[own_rows]

    def along_outer(layer, way, source=None):
        where = rows_of(at(layer, x), 0, piece)
        source = gathered(where) if source is None else source
        return copy_pair(
            source, where, at(z + way, x), send_outer.at[layer, (way + 1) // 2], recv_sem.at[at(layer, x)]
        )

    def along_inner(layer, step, count, source=None):
        where = rows_of(at(layer, x), 0, count)
        source = gathered(where) if source is None else source
        return copy_pair(
            source, where, at(z, lax.rem(x + step, inner)), send_inner.at[layer, step - 1], recv_sem.at[at(layer, x)]
        )

    def extra(end, way):
        layer = end * (outer - 1)
        where = rows_of(at(layer, 1 - x), half, half)
        return copy_pair(gathered(where), where, at(z + way, x), extra_send.at[end], extra_recv.at[end])

    def start(copies):
        for copy in copies:
            copy.start()

    def wait_send(copies):
        for copy in copies:
            copy.wait_send()

    def wait_recv(index, offset, count, sem):
        where = rows_of(index, offset, count)
        for which, dst in enumerate((all_points, all_probes)):
            pltpu.make_async_copy(dst.at[where], dst.at[where], sem.at[which]).wait()

    def is_end(layer):
        return (layer == 0) | (layer == outer - 1)

    def inside(layer):
        return (layer >= 0) & (layer < outer)

    def pair(visitor, visitor_probes):
        visitor_sq = jnp.sum(visitor * visitor, axis=1, keepdims=True)
        cross = lax.dot_general(
            visitor,
            own[...],
            (((1,), (1,)), ((), ())),
            precision=HIGHEST,
            preferred_element_type=jnp.float32,
        )
        arg = (visitor_sq + own_sq[...] - 2.0 * cross) * scale
        value = jnp.exp(-jnp.maximum(arg, 0.0))
        total[...] += jnp.dot(
            value.T, visitor_probes, precision=HIGHEST, preferred_element_type=jnp.float32
        )

    def pair_at(index, offset, count):
        where = rows_of(index, offset, count)
        pair(all_points[where, :], all_probes[where, :])

    barrier = pltpu.get_barrier_semaphore()
    for way in (1, -1):
        @pl.when(inside(z + way))
        def _(way=way):
            pl.semaphore_signal(barrier, inc=1, device_id={"blk": at(z + way, x)}, device_id_type=MESH)
    for step in range(1, inner):
        pl.semaphore_signal(
            barrier, inc=1, device_id={"blk": at(z, lax.rem(x + step, inner))}, device_id_type=MESH
        )
    for step in range(1, team_size):
        pl.semaphore_signal(
            barrier, inc=1, device_id={"team": lax.rem(team + step, team_size)}, device_id_type=MESH
        )
    loads = [
        pltpu.make_async_copy(points_hbm, own, load_sem.at[0]),
        pltpu.make_async_copy(probes_hbm, own_probes, load_sem.at[1]),
    ]
    start(loads)
    neighbours = jnp.where(z > 0, 1, 0) + jnp.where(z < outer - 1, 1, 0)
    pl.semaphore_wait(barrier, neighbours + inner - 1 + team_size - 1)

    for way in (1, -1):
        @pl.when(inside(z + way))
        def _(way=way):
            start(along_outer(z, way, own_source))
    for step in range(1, inner):
        start(along_inner(z, step, piece, own_source))

    for load in loads:
        load.wait()
    column = jnp.sum(own[...] * own[...], axis=1, keepdims=True)
    own_sq[...] = jnp.broadcast_to(column, (rows, 128)).T[0:1, :]
    total[...] = jnp.zeros_like(total)
    pair(own[own_rows, :], own_probes[own_rows, :])

    def from_inner(layer):
        for step in range(1, inner):
            index = at(layer, lax.rem(x + step, inner))
            if split:
                @pl.when(is_end(layer) & (layer != z))
                def _():
                    wait_recv(index, 0, half, recv_sem.at[index])
                    pair_at(index, 0, half)

                @pl.when(jnp.logical_not(is_end(layer) & (layer != z)))
                def _():
                    wait_recv(index, 0, piece, recv_sem.at[index])
            else:
                wait_recv(index, 0, piece, recv_sem.at[index])

    def pair_inner(layer):
        for step in range(1, inner):
            index = at(layer, lax.rem(x + step, inner))
            if split:
                @pl.when(jnp.logical_not(is_end(layer) & (layer != z)))
                def _():
                    pair_at(index, 0, piece)
            else:
                pair_at(index, 0, piece)

    def from_extra(layer, way):
        end = layer // (outer - 1)
        index = at(layer, 1 - x)
        wait_recv(index, half, half, extra_recv.at[end])

        @pl.when(inside(z - way))
        def _():
            start(extra(end, -way))
        pair_at(index, half, half)

    def arrive(k, carry):
        d = k // 2 + 1
        way = 1 - 2 * lax.rem(k, 2)
        layer = z + way * d

        @pl.when(inside(layer))
        def _():
            wait_recv(at(layer, x), 0, piece, recv_sem.at[at(layer, x)])

            @pl.when(inside(z - way))
            def _():
                start(along_outer(layer, -way))

            for step in range(1, inner):
                if split:
                    @pl.when(is_end(layer))
                    def _():
                        start(along_inner(layer, step, half))

                    @pl.when(jnp.logical_not(is_end(layer)))
                    def _():
                        start(along_inner(layer, step, piece))
                else:
                    start(along_inner(layer, step, piece))
            pair_at(at(layer, x), 0, piece)

        before = z + way * (d - 1)

        @pl.when(inside(before) & ((d > 1) | (way > 0)))
        def _():
            from_inner(before)
            if split:
                @pl.when((d == 1) & is_end(z))
                def _():
                    start(extra(z // (outer - 1), 1 - 2 * (z // (outer - 1))))
            pair_inner(before)
        if split:
            @pl.when(inside(before) & is_end(before) & (before != z))
            def _():
                from_extra(before, way)
        return carry

    lax.fori_loop(0, 2 * (outer - 1), arrive, 0)
    for way in (1, -1):
        last = z + way * (outer - 1)

        @pl.when(inside(last))
        def _(last=last, way=way):
            from_inner(last)
            pair_inner(last)
            if split:
                from_extra(last, way)

    def part(step):
        peer = lax.rem(team + step, team_size)
        return pltpu.make_async_remote_copy(
            src_ref=total.at[pl.ds(pl.multiple_of(peer * piece, piece), piece)],
            dst_ref=parts.at[step - 1],
            send_sem=part_send.at[step - 1],
            recv_sem=part_recv.at[step - 1],
            device_id={"team": peer},
            device_id_type=MESH,
        )

    for step in range(1, team_size):
        part(step).start()
    for way in (1, -1):
        @pl.when(inside(z + way))
        def _(way=way):
            wait_send(along_outer(z, way, own_source))
    for step in range(1, inner):
        wait_send(along_inner(z, step, piece, own_source))

    def sent(k, carry):
        d = k // 2 + 1
        way = 1 - 2 * lax.rem(k, 2)
        layer = z + way * d

        @pl.when(inside(layer))
        def _():
            @pl.when(inside(z - way))
            def _():
                wait_send(along_outer(layer, -way))

            for step in range(1, inner):
                if split:
                    @pl.when(is_end(layer))
                    def _():
                        wait_send(along_inner(layer, step, half))

                    @pl.when(jnp.logical_not(is_end(layer)))
                    def _():
                        wait_send(along_inner(layer, step, piece))
                else:
                    wait_send(along_inner(layer, step, piece))
            if split:
                @pl.when(is_end(layer) & inside(z - way))
                def _():
                    wait_send(extra(layer // (outer - 1), -way))
        return carry

    lax.fori_loop(0, 2 * (outer - 1), sent, 0)
    if split:
        @pl.when(is_end(z))
        def _():
            wait_send(extra(z // (outer - 1), 1 - 2 * (z // (outer - 1))))
    result = total[own_rows, :]
    for step in range(1, team_size):
        part(step).wait_recv()
        result = result + parts[step - 1]
    out_ref[...] = result
    for step in range(1, team_size):
        part(step).wait_send()


def body(points, probes):
    rows, width = points.shape
    count = probes.shape[1]
    team_size = lax.axis_size("team")
    blocks = lax.axis_size("blk")
    inner = 1 << ((blocks.bit_length() - 1) // 2)
    outer = blocks // inner
    piece = rows // team_size
    f32 = jnp.float32
    dma = pltpu.SemaphoreType.DMA
    return pl.pallas_call(
        functools.partial(kernel, blocks, outer, inner, team_size),
        out_shape=jax.ShapeDtypeStruct((piece, count), f32),
        in_specs=[pl.BlockSpec(memory_space=pl.ANY)] * 2,
        out_specs=pl.BlockSpec(memory_space=pltpu.VMEM),
        scratch_shapes=[
            pltpu.VMEM((rows, width), f32),
            pltpu.VMEM((rows, count), f32),
            pltpu.VMEM((blocks * piece, width), f32),
            pltpu.VMEM((blocks * piece, count), f32),
            pltpu.VMEM((1, rows), f32),
            pltpu.VMEM((rows, count), f32),
            pltpu.VMEM((team_size - 1, piece, count), f32),
            dma((2,)),
            dma((blocks, 2)),
            dma((2, 2)),
            dma((outer, 2, 2)),
            dma((outer, max(inner - 1, 1), 2)),
            dma((2, 2)),
            dma((team_size - 1,)),
            dma((team_size - 1,)),
        ],
        compiler_params=pltpu.CompilerParams(collective_id=0, has_side_effects=True),
    )(points, probes)


def solution(mesh):
    in_specs = (P("blk", None), P("blk", None))
    out_specs = P(("blk", "team"), None)
    return jax.shard_map(body, mesh=mesh, in_specs=in_specs, out_specs=out_specs, check_vma=False)
```

```python
import functools

import jax
import jax.numpy as jnp
from jax import lax
from jax.experimental import pallas as pl
from jax.experimental.pallas import tpu as pltpu
from jax.sharding import PartitionSpec as P

HIGHEST = lax.Precision.HIGHEST
MESH = pl.DeviceIdType.MESH


def kernel(
    outer,
    inner,
    points_hbm,
    probes_hbm,
    out_ref,
    layer_points,
    layer_probes,
    layer_sq,
    visitors,
    sums,
    returned,
    load_sem,
    visit_send,
    visit_recv,
    row_send,
    share_send,
    row_recv,
    back_send,
    back_recv,
):
    rows, width = points_hbm.shape
    piece = visitors.shape[1]
    half = rows // 2
    sub = half // 2
    scale = 2.0 / width
    block = lax.axis_index("blk")
    team = lax.axis_index("team")
    z = block // inner
    x = lax.rem(block, inner)
    core = lax.rem(team, 2)
    sibling = {"team": team + 1 - 2 * core}

    def at(layer, column):
        return {"blk": layer * inner + column}

    def inside(layer):
        return (layer >= 0) & (layer < outer)

    def remote(src, dst, send, recv, target):
        return pltpu.make_async_remote_copy(
            src_ref=src, dst_ref=dst, send_sem=send, recv_sem=recv, device_id=target, device_id_type=MESH
        )

    def wait_recv(ref, sem):
        pltpu.make_async_copy(ref, ref, sem).wait()

    own_rows = pl.ds(pl.multiple_of(team * piece, piece), piece)

    def onward(layer, way, source=None):
        return remote(
            visitors.at[layer] if source is None else source,
            visitors.at[layer],
            visit_send.at[layer, (way + 1) // 2],
            visit_recv.at[layer],
            at(z + way, x),
        )

    def slot(column, part, side):
        return (column * 2 + part) * 2 + side

    def slot_rows(column, part, side):
        return pl.ds(pl.multiple_of(column * rows + part * half + side * sub, sub), sub)

    def across(step, part):
        source = pl.ds(pl.multiple_of(part * half + core * sub, sub), sub)
        where = slot_rows(x, part, core)
        return [
            remote(
                src.at[source],
                dst.at[where],
                row_send.at[step - 1, part, which],
                row_recv.at[slot(x, part, core), which],
                at(z, lax.rem(x + step, inner)),
            )
            for which, (src, dst) in enumerate(((points_hbm, layer_points), (probes_hbm, layer_probes)))
        ]

    def share(step, part):
        column = lax.rem(x + step, inner)
        where = slot_rows(column, part, core)
        return [
            remote(
                ref.at[where],
                ref.at[where],
                share_send.at[step - 1, part, which],
                row_recv.at[slot(column, part, core), which],
                sibling,
            )
            for which, ref in enumerate((layer_points, layer_probes))
        ]

    def wait_rows(column, part, side):
        for which, ref in enumerate((layer_points, layer_probes)):
            wait_recv(ref.at[slot_rows(column, part, side)], row_recv.at[slot(column, part, side), which])

    def back(layer):
        return remote(sums.at[layer], returned.at[z], back_send.at[layer], back_recv.at[z], at(layer, x))

    def half_rows(column, part):
        return pl.ds(pl.multiple_of(column * rows + part * half, half), half)

    def square(column, part):
        values = layer_points[half_rows(column, part), :]
        total = jnp.sum(values * values, axis=1, keepdims=True)
        layer_sq[column * 2 + part] = jnp.broadcast_to(total, (half, 128)).T[0:1, :]

    def pair(layer, column, parts, fresh=False):
        first = parts[0]
        where = pl.ds(pl.multiple_of(column * rows + first * half, half), half * len(parts))
        visitor = visitors[layer]
        visitor_sq = jnp.sum(visitor * visitor, axis=1, keepdims=True)
        cross = lax.dot_general(
            visitor,
            layer_points[where, :],
            (((1,), (1,)), ((), ())),
            precision=HIGHEST,
            preferred_element_type=jnp.float32,
        )
        row_sq = jnp.concatenate([layer_sq[column * 2 + part] for part in parts], axis=1)
        arg = (visitor_sq + row_sq - 2.0 * cross) * scale
        value = jnp.exp(-jnp.maximum(arg, 0.0))
        product = jnp.dot(
            value, layer_probes[where, :], precision=HIGHEST, preferred_element_type=jnp.float32
        )
        sums[layer] = product if fresh else sums[layer] + product

    barrier = pltpu.get_barrier_semaphore()
    for step in range(1, outer):
        pl.semaphore_signal(barrier, inc=1, device_id=at(lax.rem(z + step, outer), x), device_id_type=MESH)
    for step in range(1, inner):
        pl.semaphore_signal(barrier, inc=1, device_id=at(z, lax.rem(x + step, inner)), device_id_type=MESH)
    pl.semaphore_signal(barrier, inc=1, device_id=sibling, device_id_type=MESH)
    mine = pl.ds(pl.multiple_of(x * rows, rows), rows)
    loads = [
        pltpu.make_async_copy(points_hbm, layer_points.at[mine], load_sem.at[0]),
        pltpu.make_async_copy(probes_hbm, layer_probes.at[mine], load_sem.at[1]),
        pltpu.make_async_copy(points_hbm.at[own_rows], visitors.at[z], load_sem.at[2]),
    ]
    for load in loads:
        load.start()
    pl.semaphore_wait(barrier, outer - 1 + inner - 1 + 1)

    for way in (1, -1):
        @pl.when(inside(z + way))
        def _(way=way):
            onward(z, way, points_hbm.at[own_rows]).start()
    for part in range(2):
        for step in range(1, inner):
            for copy in across(step, part):
                copy.start()

    for load in loads:
        load.wait()
    square(x, 0)
    square(x, 1)
    pair(z, x, (0, 1), fresh=True)

    def both_ways(distance, work):
        def one(k, carry):
            layer = z + (1 - 2 * k) * distance

            @pl.when(inside(layer))
            def _():
                work(layer, 1 - 2 * k)
            return carry
        lax.fori_loop(0, 2, one, 0)

    def receive(layer, way):
        wait_recv(visitors.at[layer], visit_recv.at[layer])

        @pl.when(inside(z - way))
        def _():
            onward(layer, -way).start()
        pair(layer, x, (0, 1), fresh=True)

    def others(work):
        def one(step, carry):
            work(step, lax.rem(x + step, inner))
            return carry
        lax.fori_loop(1, inner, one, 0)

    def take_rows(part, reach):
        def take(step, column):
            wait_rows(column, part, core)
            for copy in share(step, part):
                copy.start()
        others(take)

        def use(step, column):
            wait_rows(column, part, 1 - core)
            square(column, part)

            def one(k, carry):
                layer = z + k - reach

                @pl.when(inside(layer))
                def _():
                    pair(layer, column, (part,))
                return carry
            lax.fori_loop(0, 2 * reach + 1, one, 0)
        others(use)

    near = min(2, outer - 1)
    both_ways(1, receive)
    take_rows(0, 1)
    if near == 2:
        def receive_more(layer, way):
            receive(layer, way)
            others(lambda step, column: pair(layer, column, (0,)))
        both_ways(2, receive_more)
    take_rows(1, near)
    for distance in range(1, near + 1):
        both_ways(distance, lambda layer, way: back(layer).start())

    def receive_all(layer, way):
        receive(layer, way)
        others(lambda step, column: pair(layer, column, (0, 1)))
        back(layer).start()
    for distance in range(near + 1, outer):
        both_ways(distance, receive_all)

    for way in (1, -1):
        @pl.when(inside(z + way))
        def _(way=way):
            onward(z, way, points_hbm.at[own_rows]).wait_send()

    def sent(layer, way):
        @pl.when(inside(z - way))
        def _():
            onward(layer, -way).wait_send()
    for distance in range(1, outer):
        both_ways(distance, sent)
    for part in range(2):
        for step in range(1, inner):
            for copy in across(step, part) + share(step, part):
                copy.wait_send()

    result = sums[z]
    for step in range(1, outer):
        layer = lax.rem(z + step, outer)
        wait_recv(returned.at[layer], back_recv.at[layer])
        result = result + returned[layer]
    out_ref[...] = result
    for step in range(1, outer):
        back(lax.rem(z + step, outer)).wait_send()


def body(points, probes):
    rows, width = points.shape
    count = probes.shape[1]
    blocks = lax.axis_size("blk")
    inner = 1 << ((blocks.bit_length() - 1) // 2)
    outer = blocks // inner
    piece = rows // lax.axis_size("team")
    f32 = jnp.float32
    dma = pltpu.SemaphoreType.DMA
    return pl.pallas_call(
        functools.partial(kernel, outer, inner),
        out_shape=jax.ShapeDtypeStruct((piece, count), f32),
        in_specs=[pl.BlockSpec(memory_space=pl.ANY)] * 2,
        out_specs=pl.BlockSpec(memory_space=pltpu.VMEM),
        scratch_shapes=[
            pltpu.VMEM((inner * rows, width), f32),
            pltpu.VMEM((inner * rows, count), f32),
            pltpu.VMEM((inner * 2, 1, rows // 2), f32),
            pltpu.VMEM((outer, piece, width), f32),
            pltpu.VMEM((outer, piece, count), f32),
            pltpu.VMEM((outer, piece, count), f32),
            dma((3,)),
            dma((outer, 2)),
            dma((outer,)),
            dma((inner - 1, 2, 2)),
            dma((inner - 1, 2, 2)),
            dma((inner * 4, 2)),
            dma((outer,)),
            dma((outer,)),
        ],
        compiler_params=pltpu.CompilerParams(collective_id=0, has_side_effects=True),
    )(points, probes)


def solution(mesh):
    in_specs = (P("blk", None), P("blk", None))
    out_specs = P(("blk", "team"), None)
    return jax.shard_map(body, mesh=mesh, in_specs=in_specs, out_specs=out_specs, check_vma=False)
```

```python
import functools

import jax
import jax.numpy as jnp
from jax import lax
from jax.experimental import pallas as pl
from jax.experimental.pallas import tpu as pltpu
from jax.sharding import PartitionSpec as P

MESH = pl.DeviceIdType.MESH


def kernel(
    outer,
    inner,
    points_hbm,
    probes_hbm,
    out_ref,
    layer_points,
    layer_probes,
    points_high,
    points_low,
    probes_high,
    probes_low,
    layer_sq,
    visitors,
    visitor_terms,
    visitor_sq,
    sums,
    returned,
    load_sem,
    visit_send,
    visit_recv,
    row_send,
    share_send,
    row_recv,
    back_send,
    back_recv,
):
    rows, width = points_hbm.shape
    piece = visitors.shape[1]
    half = rows // 2
    sub = half // 2
    scale = 2.0 / width
    block = lax.axis_index("blk")
    team = lax.axis_index("team")
    z = block // inner
    x = lax.rem(block, inner)
    core = lax.rem(team, 2)
    sibling = {"team": team + 1 - 2 * core}

    def at(layer, column):
        return {"blk": layer * inner + column}

    def inside(layer):
        return (layer >= 0) & (layer < outer)

    def remote(src, dst, send, recv, target):
        return pltpu.make_async_remote_copy(
            src_ref=src, dst_ref=dst, send_sem=send, recv_sem=recv, device_id=target, device_id_type=MESH
        )

    def wait_recv(ref, sem):
        pltpu.make_async_copy(ref, ref, sem).wait()

    own_rows = pl.ds(pl.multiple_of(team * piece, piece), piece)

    def onward(layer, way, turn, first=False):
        where = pl.ds(turn * (piece // 2), piece // 2)
        return remote(
            points_hbm.at[pl.ds(pl.multiple_of(team * piece + turn * (piece // 2), piece // 2), piece // 2)]
            if first
            else visitors.at[layer, where],
            visitors.at[layer, where],
            visit_send.at[layer, (way + 1) // 2, turn],
            visit_recv.at[layer, turn],
            at(z + way, x),
        )

    def slot(column, part, side):
        return (column * 2 + part) * 2 + side

    def slot_rows(column, part, side):
        return pl.ds(pl.multiple_of(column * rows + part * half + side * sub, sub), sub)

    def across(step, part):
        source = pl.ds(pl.multiple_of(part * half + core * sub, sub), sub)
        where = slot_rows(x, part, core)
        return [
            remote(
                src.at[source],
                dst.at[where],
                row_send.at[step - 1, part, which],
                row_recv.at[slot(x, part, core), which],
                at(z, lax.rem(x + step, inner)),
            )
            for which, (src, dst) in enumerate(((points_hbm, layer_points), (probes_hbm, layer_probes)))
        ]

    def share(step, part):
        column = lax.rem(x + step, inner)
        where = slot_rows(column, part, core)
        return [
            remote(
                ref.at[where],
                ref.at[where],
                share_send.at[step - 1, part, which],
                row_recv.at[slot(column, part, core), which],
                sibling,
            )
            for which, ref in enumerate((layer_points, layer_probes))
        ]

    def wait_rows(column, part, side):
        for which, ref in enumerate((layer_points, layer_probes)):
            wait_recv(ref.at[slot_rows(column, part, side)], row_recv.at[slot(column, part, side), which])

    def back(layer):
        return remote(sums.at[layer], returned.at[z], back_send.at[layer], back_recv.at[z], at(layer, x))

    def half_rows(column, part):
        return pl.ds(pl.multiple_of(column * rows + part * half, half), half)

    def two_terms(values):
        high = values.astype(jnp.bfloat16)
        return high, (values - high.astype(jnp.float32)).astype(jnp.bfloat16)

    def four_products(stacked, high, low, contract):
        count = stacked.shape[0] // 2
        dot = functools.partial(
            lax.dot_general,
            dimension_numbers=(contract, ((), ())),
            preferred_element_type=jnp.float32,
        )
        by_high, by_low = dot(stacked, high), dot(stacked, low)
        return by_high[:count] + (by_high[count:] + by_low[:count] + by_low[count:])

    def prepare_rows(column, part):
        where = half_rows(column, part)
        values = layer_points[where, :]
        total = jnp.sum(values * values, axis=1, keepdims=True)
        layer_sq[column * 2 + part] = jnp.broadcast_to(total, (half, 128)).T[0:1, :]
        points_high[where, :], points_low[where, :] = two_terms(values)
        probes_high[where, :], probes_low[where, :] = two_terms(layer_probes[where, :])

    def prepare_visitor(layer):
        values = visitors[layer]
        visitor_sq[layer] = jnp.sum(values * values, axis=1, keepdims=True)
        high, low = two_terms(values)
        visitor_terms[layer, 0:piece, :] = high
        visitor_terms[layer, piece : 2 * piece, :] = low

    def pair(layer, column, parts, fresh=False):
        first = parts[0]
        where = pl.ds(pl.multiple_of(column * rows + first * half, half), half * len(parts))
        cross = four_products(
            visitor_terms[layer], points_high[where, :], points_low[where, :], ((1,), (1,))
        )
        row_sq = jnp.concatenate([layer_sq[column * 2 + part] for part in parts], axis=1)
        arg = (visitor_sq[layer] + row_sq - 2.0 * cross) * scale
        value = jnp.exp(-jnp.maximum(arg, 0.0))
        product = four_products(
            jnp.concatenate(two_terms(value), axis=0),
            probes_high[where, :],
            probes_low[where, :],
            ((1,), (0,)),
        )
        sums[layer] = product if fresh else sums[layer] + product

    barrier = pltpu.get_barrier_semaphore()
    for step in range(1, outer):
        pl.semaphore_signal(barrier, inc=1, device_id=at(lax.rem(z + step, outer), x), device_id_type=MESH)
    for step in range(1, inner):
        pl.semaphore_signal(barrier, inc=1, device_id=at(z, lax.rem(x + step, inner)), device_id_type=MESH)
    pl.semaphore_signal(barrier, inc=1, device_id=sibling, device_id_type=MESH)
    mine = pl.ds(pl.multiple_of(x * rows, rows), rows)
    loads = [
        pltpu.make_async_copy(points_hbm, layer_points.at[mine], load_sem.at[0]),
        pltpu.make_async_copy(probes_hbm, layer_probes.at[mine], load_sem.at[1]),
        pltpu.make_async_copy(points_hbm.at[own_rows], visitors.at[z], load_sem.at[2]),
    ]
    for load in loads:
        load.start()
    pl.semaphore_wait(barrier, outer - 1 + inner - 1 + 1)

    for way in (1, -1):
        @pl.when(inside(z + way))
        def _(way=way):
            onward(z, way, 0, first=True).start()
            onward(z, way, 1, first=True).start()
    for part in range(2):
        for step in range(1, inner):
            for copy in across(step, part):
                copy.start()

    for load in loads:
        load.wait()
    prepare_rows(x, 0)
    prepare_rows(x, 1)
    prepare_visitor(z)
    pair(z, x, (0, 1), fresh=True)

    def both_ways(distance, work):
        def one(k, carry):
            layer = z + (1 - 2 * k) * distance

            @pl.when(inside(layer))
            def _():
                work(layer, 1 - 2 * k)
            return carry
        lax.fori_loop(0, 2, one, 0)

    def receive(distance, turn):
        def work(layer, way):
            wait_recv(visitors.at[layer, pl.ds(turn * (piece // 2), piece // 2)], visit_recv.at[layer, turn])

            @pl.when(inside(z - way))
            def _():
                onward(layer, -way, turn).start()
        both_ways(distance, work)

    def others(work):
        def one(step, carry):
            work(step, lax.rem(x + step, inner))
            return carry
        lax.fori_loop(1, inner, one, 0)

    def take_rows(part):
        def take(step, column):
            wait_rows(column, part, core)
            for copy in share(step, part):
                copy.start()
        others(take)

    def use_rows(part, reach):
        def use(step, column):
            wait_rows(column, part, 1 - core)
            prepare_rows(column, part)

            def one(k, carry):
                layer = z + k - reach

                @pl.when(inside(layer))
                def _():
                    pair(layer, column, (part,))
                return carry
            lax.fori_loop(0, 2 * reach + 1, one, 0)
        others(use)

    def meet_own(layer, way):
        prepare_visitor(layer)
        pair(layer, x, (0, 1), fresh=True)

    near = min(2, outer - 1)
    receive(1, 0)
    receive(1, 1)
    both_ways(1, meet_own)
    take_rows(0)
    if near == 2:
        receive(2, 0)
    use_rows(0, 1)
    if near == 2:
        receive(2, 1)

        def meet_more(layer, way):
            meet_own(layer, way)
            others(lambda step, column: pair(layer, column, (0,)))
        both_ways(2, meet_more)
    take_rows(1)
    use_rows(1, near)
    for distance in range(1, near + 1):
        both_ways(distance, lambda layer, way: back(layer).start())

    def meet_all(layer, way):
        meet_own(layer, way)
        others(lambda step, column: pair(layer, column, (0, 1)))
        back(layer).start()
    for distance in range(near + 1, outer):
        receive(distance, 0)
        receive(distance, 1)
        both_ways(distance, meet_all)

    for way in (1, -1):
        @pl.when(inside(z + way))
        def _(way=way):
            onward(z, way, 0, first=True).wait_send()
            onward(z, way, 1, first=True).wait_send()

    def sent(layer, way):
        @pl.when(inside(z - way))
        def _():
            onward(layer, -way, 0).wait_send()
            onward(layer, -way, 1).wait_send()
    for distance in range(1, outer):
        both_ways(distance, sent)
    for part in range(2):
        for step in range(1, inner):
            for copy in across(step, part) + share(step, part):
                copy.wait_send()

    result = sums[z]
    for step in range(1, outer):
        layer = lax.rem(z + step, outer)
        wait_recv(returned.at[layer], back_recv.at[layer])
        result = result + returned[layer]
    out_ref[...] = result
    for step in range(1, outer):
        back(lax.rem(z + step, outer)).wait_send()


def body(points, probes):
    rows, width = points.shape
    count = probes.shape[1]
    blocks = lax.axis_size("blk")
    inner = 1 << ((blocks.bit_length() - 1) // 2)
    outer = blocks // inner
    piece = rows // lax.axis_size("team")
    f32, bf16 = jnp.float32, jnp.bfloat16
    dma = pltpu.SemaphoreType.DMA
    return pl.pallas_call(
        functools.partial(kernel, outer, inner),
        out_shape=jax.ShapeDtypeStruct((piece, count), f32),
        in_specs=[pl.BlockSpec(memory_space=pl.ANY)] * 2,
        out_specs=pl.BlockSpec(memory_space=pltpu.VMEM),
        scratch_shapes=[
            pltpu.VMEM((inner * rows, width), f32),
            pltpu.VMEM((inner * rows, count), f32),
            pltpu.VMEM((inner * rows, width), bf16),
            pltpu.VMEM((inner * rows, width), bf16),
            pltpu.VMEM((inner * rows, count), bf16),
            pltpu.VMEM((inner * rows, count), bf16),
            pltpu.VMEM((inner * 2, 1, rows // 2), f32),
            pltpu.VMEM((outer, piece, width), f32),
            pltpu.VMEM((outer, 2 * piece, width), bf16),
            pltpu.VMEM((outer, piece, 1), f32),
            pltpu.VMEM((outer, piece, count), f32),
            pltpu.VMEM((outer, piece, count), f32),
            dma((3,)),
            dma((outer, 2, 2)),
            dma((outer, 2)),
            dma((inner - 1, 2, 2)),
            dma((inner - 1, 2, 2)),
            dma((inner * 4, 2)),
            dma((outer,)),
            dma((outer,)),
        ],
        compiler_params=pltpu.CompilerParams(collective_id=0, has_side_effects=True),
    )(points, probes)


def solution(mesh):
    in_specs = (P("blk", None), P("blk", None))
    out_specs = P(("blk", "team"), None)
    return jax.shard_map(body, mesh=mesh, in_specs=in_specs, out_specs=out_specs, check_vma=False)
```

```python
import functools

import jax
import jax.numpy as jnp
from jax import lax
from jax.experimental import pallas as pl
from jax.experimental.pallas import tpu as pltpu
from jax.sharding import PartitionSpec as P

MESH = pl.DeviceIdType.MESH


def kernel(
    outer,
    inner,
    points_hbm,
    probes_hbm,
    out_ref,
    layer_points,
    layer_probes,
    points_high,
    points_low,
    probes_high,
    probes_low,
    layer_sq,
    visitors,
    visitor_terms,
    visitor_sq,
    sums,
    returned,
    load_sem,
    visit_send,
    visit_recv,
    row_send,
    share_send,
    row_recv,
    back_send,
    back_recv,
):
    rows, width = points_hbm.shape
    piece = visitors.shape[1]
    half = rows // 2
    sub = half // 2
    scale = 2.0 / width
    block = lax.axis_index("blk")
    team = lax.axis_index("team")
    z = block // inner
    x = lax.rem(block, inner)
    core = lax.rem(team, 2)
    sibling = {"team": team + 1 - 2 * core}

    def at(layer, column):
        return {"blk": layer * inner + column}

    def inside(layer):
        return (layer >= 0) & (layer < outer)

    def remote(src, dst, send, recv, target):
        return pltpu.make_async_remote_copy(
            src_ref=src, dst_ref=dst, send_sem=send, recv_sem=recv, device_id=target, device_id_type=MESH
        )

    def wait_recv(ref, sem):
        pltpu.make_async_copy(ref, ref, sem).wait()

    own_rows = pl.ds(pl.multiple_of(team * piece, piece), piece)

    def onward(layer, way, turn, first=False):
        where = pl.ds(turn * (piece // 2), piece // 2)
        return remote(
            points_hbm.at[pl.ds(pl.multiple_of(team * piece + turn * (piece // 2), piece // 2), piece // 2)]
            if first
            else visitors.at[layer, where],
            visitors.at[layer, where],
            visit_send.at[layer, (way + 1) // 2, turn],
            visit_recv.at[layer, turn],
            at(z + way, x),
        )

    def slot(column, part, side):
        return (column * 2 + part) * 2 + side

    def slot_rows(column, part, side):
        return pl.ds(pl.multiple_of(column * rows + part * half + side * sub, sub), sub)

    def across(step, part):
        source = pl.ds(pl.multiple_of(part * half + core * sub, sub), sub)
        where = slot_rows(x, part, core)
        return [
            remote(
                src.at[source],
                dst.at[where],
                row_send.at[step - 1, part, which],
                row_recv.at[slot(x, part, core), which],
                at(z, lax.rem(x + step, inner)),
            )
            for which, (src, dst) in enumerate(((points_hbm, layer_points), (probes_hbm, layer_probes)))
        ]

    def share(step, part):
        column = lax.rem(x + step, inner)
        where = slot_rows(column, part, core)
        return [
            remote(
                ref.at[where],
                ref.at[where],
                share_send.at[step - 1, part, which],
                row_recv.at[slot(column, part, core), which],
                sibling,
            )
            for which, ref in enumerate((layer_points, layer_probes))
        ]

    def wait_rows(column, part, side):
        for which, ref in enumerate((layer_points, layer_probes)):
            wait_recv(ref.at[slot_rows(column, part, side)], row_recv.at[slot(column, part, side), which])

    def back(layer, turn):
        where = pl.ds(turn * (piece // 2), piece // 2)
        return remote(
            sums.at[layer, where],
            returned.at[z, where],
            back_send.at[layer, turn],
            back_recv.at[z, turn],
            at(layer, x),
        )

    def half_rows(column, part):
        return pl.ds(pl.multiple_of(column * rows + part * half, half), half)

    def two_terms(values):
        high = values.astype(jnp.bfloat16)
        return high, (values - high.astype(jnp.float32)).astype(jnp.bfloat16)

    def four_products(stacked, high, low, contract):
        count = stacked.shape[0] // 2
        dot = functools.partial(
            lax.dot_general,
            dimension_numbers=(contract, ((), ())),
            preferred_element_type=jnp.float32,
        )
        by_high, by_low = dot(stacked, high), dot(stacked, low)
        return by_high[:count] + (by_high[count:] + by_low[:count] + by_low[count:])

    def prepare_rows(column, part):
        where = half_rows(column, part)
        values = layer_points[where, :]
        total = jnp.sum(values * values, axis=1, keepdims=True)
        layer_sq[column * 2 + part] = jnp.broadcast_to(total, (half, 128)).T[0:1, :]
        points_high[where, :], points_low[where, :] = two_terms(values)
        probes_high[where, :], probes_low[where, :] = two_terms(layer_probes[where, :])

    def prepare_visitor(layer, begin=0, count=piece):
        values = visitors[layer, begin : begin + count, :]
        visitor_sq[layer, begin : begin + count] = jnp.sum(values * values, axis=1, keepdims=True)
        high, low = two_terms(values)
        visitor_terms[layer, begin : begin + count, :] = high
        visitor_terms[layer, piece + begin : piece + begin + count, :] = low

    def pair(layer, column, parts, fresh=False, begin=0, count=piece):
        first = parts[0]
        where = pl.ds(pl.multiple_of(column * rows + first * half, half), half * len(parts))
        cross = four_products(
            jnp.concatenate(
                [
                    visitor_terms[layer, begin : begin + count, :],
                    visitor_terms[layer, piece + begin : piece + begin + count, :],
                ],
                axis=0,
            ),
            points_high[where, :],
            points_low[where, :],
            ((1,), (1,)),
        )
        row_sq = jnp.concatenate([layer_sq[column * 2 + part] for part in parts], axis=1)
        arg = (visitor_sq[layer, begin : begin + count] + row_sq - 2.0 * cross) * scale
        value = jnp.exp(-jnp.maximum(arg, 0.0))
        product = four_products(
            jnp.concatenate(two_terms(value), axis=0),
            probes_high[where, :],
            probes_low[where, :],
            ((1,), (0,)),
        )
        kept = slice(begin, begin + count)
        sums[layer, kept, :] = product if fresh else sums[layer, kept, :] + product

    barrier = pltpu.get_barrier_semaphore()
    for step in range(1, outer):
        pl.semaphore_signal(barrier, inc=1, device_id=at(lax.rem(z + step, outer), x), device_id_type=MESH)
    for step in range(1, inner):
        pl.semaphore_signal(barrier, inc=1, device_id=at(z, lax.rem(x + step, inner)), device_id_type=MESH)
    pl.semaphore_signal(barrier, inc=1, device_id=sibling, device_id_type=MESH)
    mine = pl.ds(pl.multiple_of(x * rows, rows), rows)
    loads = [
        pltpu.make_async_copy(points_hbm, layer_points.at[mine], load_sem.at[0]),
        pltpu.make_async_copy(probes_hbm, layer_probes.at[mine], load_sem.at[1]),
        pltpu.make_async_copy(points_hbm.at[own_rows], visitors.at[z], load_sem.at[2]),
    ]
    for load in loads:
        load.start()
    pl.semaphore_wait(barrier, outer - 1 + inner - 1 + 1)

    for way in (1, -1):
        @pl.when(inside(z + way))
        def _(way=way):
            onward(z, way, 0, first=True).start()
            onward(z, way, 1, first=True).start()
    for part in range(2):
        for step in range(1, inner):
            for copy in across(step, part):
                copy.start()

    for load in loads:
        load.wait()
    prepare_rows(x, 0)
    prepare_rows(x, 1)
    prepare_visitor(z)
    pair(z, x, (0, 1), fresh=True)

    def both_ways(distance, work):
        def one(k, carry):
            layer = z + (1 - 2 * k) * distance

            @pl.when(inside(layer))
            def _():
                work(layer, 1 - 2 * k)
            return carry
        lax.fori_loop(0, 2, one, 0)

    def receive(distance, turn):
        def work(layer, way):
            wait_recv(visitors.at[layer, pl.ds(turn * (piece // 2), piece // 2)], visit_recv.at[layer, turn])

            @pl.when(inside(z - way))
            def _():
                onward(layer, -way, turn).start()
        both_ways(distance, work)

    def others(work):
        def one(step, carry):
            work(step, lax.rem(x + step, inner))
            return carry
        lax.fori_loop(1, inner, one, 0)

    def take_rows(part):
        def take(step, column):
            wait_rows(column, part, core)
            for copy in share(step, part):
                copy.start()
        others(take)

    def use_rows(part, reach):
        def use(step, column):
            wait_rows(column, part, 1 - core)
            prepare_rows(column, part)

            def one(k, carry):
                layer = z + k - reach

                @pl.when(inside(layer))
                def _():
                    pair(layer, column, (part,))
                return carry
            lax.fori_loop(0, 2 * reach + 1, one, 0)
        others(use)

    def meet_own(layer, way):
        prepare_visitor(layer)
        pair(layer, x, (0, 1), fresh=True)

    near = min(2, outer - 1)
    receive(1, 0)
    receive(1, 1)
    both_ways(1, meet_own)
    take_rows(0)
    if near == 2:
        receive(2, 0)
    use_rows(0, 1)
    if near == 2:
        receive(2, 1)

        def meet_more(layer, way):
            meet_own(layer, way)
            others(lambda step, column: pair(layer, column, (0,)))
        both_ways(2, meet_more)
    take_rows(1)
    use_rows(1, near)
    for distance in range(1, near + 1):
        for turn in range(2):
            both_ways(distance, lambda layer, way, turn=turn: back(layer, turn).start())

    def meet_all(layer, turn):
        here = dict(begin=turn * (piece // 2), count=piece // 2)
        prepare_visitor(layer, **here)
        for column in range(0, inner, 2):
            pair(layer, column, (0, 1, 2, 3), fresh=column == 0, **here)
        back(layer, turn).start()
    for distance in range(near + 1, outer):
        for turn in range(2):
            receive(distance, turn)
            both_ways(distance, lambda layer, way, turn=turn: meet_all(layer, turn))

    for way in (1, -1):
        @pl.when(inside(z + way))
        def _(way=way):
            onward(z, way, 0, first=True).wait_send()
            onward(z, way, 1, first=True).wait_send()

    def sent(layer, way):
        @pl.when(inside(z - way))
        def _():
            onward(layer, -way, 0).wait_send()
            onward(layer, -way, 1).wait_send()
    for distance in range(1, outer):
        both_ways(distance, sent)
    for part in range(2):
        for step in range(1, inner):
            for copy in across(step, part) + share(step, part):
                copy.wait_send()

    result = sums[z]
    for step in range(1, outer):
        layer = lax.rem(z + step, outer)
        for turn in range(2):
            wait_recv(returned.at[layer, pl.ds(turn * (piece // 2), piece // 2)], back_recv.at[layer, turn])
        result = result + returned[layer]
    out_ref[...] = result
    for step in range(1, outer):
        for turn in range(2):
            back(lax.rem(z + step, outer), turn).wait_send()


def body(points, probes):
    rows, width = points.shape
    count = probes.shape[1]
    blocks = lax.axis_size("blk")
    inner = 1 << ((blocks.bit_length() - 1) // 2)
    outer = blocks // inner
    piece = rows // lax.axis_size("team")
    f32, bf16 = jnp.float32, jnp.bfloat16
    dma = pltpu.SemaphoreType.DMA
    return pl.pallas_call(
        functools.partial(kernel, outer, inner),
        out_shape=jax.ShapeDtypeStruct((piece, count), f32),
        in_specs=[pl.BlockSpec(memory_space=pl.ANY)] * 2,
        out_specs=pl.BlockSpec(memory_space=pltpu.VMEM),
        scratch_shapes=[
            pltpu.VMEM((inner * rows, width), f32),
            pltpu.VMEM((inner * rows, count), f32),
            pltpu.VMEM((inner * rows, width), bf16),
            pltpu.VMEM((inner * rows, width), bf16),
            pltpu.VMEM((inner * rows, count), bf16),
            pltpu.VMEM((inner * rows, count), bf16),
            pltpu.VMEM((inner * 2, 1, rows // 2), f32),
            pltpu.VMEM((outer, piece, width), f32),
            pltpu.VMEM((outer, 2 * piece, width), bf16),
            pltpu.VMEM((outer, piece, 1), f32),
            pltpu.VMEM((outer, piece, count), f32),
            pltpu.VMEM((outer, piece, count), f32),
            dma((3,)),
            dma((outer, 2, 2)),
            dma((outer, 2)),
            dma((inner - 1, 2, 2)),
            dma((inner - 1, 2, 2)),
            dma((inner * 4, 2)),
            dma((outer, 2)),
            dma((outer, 2)),
        ],
        compiler_params=pltpu.CompilerParams(collective_id=0, has_side_effects=True),
    )(points, probes)


def solution(mesh):
    in_specs = (P("blk", None), P("blk", None))
    out_specs = P(("blk", "team"), None)
    return jax.shard_map(body, mesh=mesh, in_specs=in_specs, out_specs=out_specs, check_vma=False)
```

```python
import functools

import jax
import jax.numpy as jnp
from jax import lax
from jax.experimental import pallas as pl
from jax.experimental.pallas import tpu as pltpu
from jax.sharding import PartitionSpec as P

MESH = pl.DeviceIdType.MESH


def kernel(
    outer,
    inner,
    points_hbm,
    probes_hbm,
    out_ref,
    layer_points,
    layer_probes,
    points_high,
    points_low,
    probes_high,
    probes_low,
    layer_sq,
    visitors,
    visitor_terms,
    visitor_sq,
    sums,
    returned,
    load_sem,
    visit_send,
    visit_recv,
    row_send,
    share_send,
    row_recv,
    back_send,
    back_recv,
):
    rows, width = points_hbm.shape
    piece = visitors.shape[1]
    half = rows // 2
    sub = half // 2
    scale = 2.0 / width
    block = lax.axis_index("blk")
    team = lax.axis_index("team")
    z = block // inner
    x = lax.rem(block, inner)
    core = lax.rem(team, 2)
    sibling = {"team": team + 1 - 2 * core}

    def at(layer, column):
        return {"blk": layer * inner + column}

    def inside(layer):
        return (layer >= 0) & (layer < outer)

    def remote(src, dst, send, recv, target):
        return pltpu.make_async_remote_copy(
            src_ref=src, dst_ref=dst, send_sem=send, recv_sem=recv, device_id=target, device_id_type=MESH
        )

    def wait_recv(ref, sem):
        pltpu.make_async_copy(ref, ref, sem).wait()

    own_rows = pl.ds(pl.multiple_of(team * piece, piece), piece)

    def onward(layer, way, turn, first=False):
        where = pl.ds(turn * (piece // 2), piece // 2)
        return remote(
            points_hbm.at[pl.ds(pl.multiple_of(team * piece + turn * (piece // 2), piece // 2), piece // 2)]
            if first
            else visitors.at[layer, where],
            visitors.at[layer, where],
            visit_send.at[layer, (way + 1) // 2, turn],
            visit_recv.at[layer, turn],
            at(z + way, x),
        )

    def slot(column, part, side):
        return (column * 2 + part) * 2 + side

    def slot_rows(column, part, side):
        return pl.ds(pl.multiple_of(column * rows + part * half + side * sub, sub), sub)

    def across(step, part):
        source = pl.ds(pl.multiple_of(part * half + core * sub, sub), sub)
        where = slot_rows(x, part, core)
        return [
            remote(
                src.at[source],
                dst.at[where],
                row_send.at[step - 1, part, which],
                row_recv.at[slot(x, part, core), which],
                at(z, lax.rem(x + step, inner)),
            )
            for which, (src, dst) in enumerate(((points_hbm, layer_points), (probes_hbm, layer_probes)))
        ]

    def share(step, part):
        column = lax.rem(x + step, inner)
        where = slot_rows(column, part, core)
        return [
            remote(
                ref.at[where],
                ref.at[where],
                share_send.at[step - 1, part, which],
                row_recv.at[slot(column, part, core), which],
                sibling,
            )
            for which, ref in enumerate((layer_points, layer_probes))
        ]

    def wait_rows(column, part, side):
        for which, ref in enumerate((layer_points, layer_probes)):
            wait_recv(ref.at[slot_rows(column, part, side)], row_recv.at[slot(column, part, side), which])

    def back(layer, turn):
        where = pl.ds(turn * (piece // 2), piece // 2)
        return remote(
            sums.at[layer, where],
            returned.at[z, where],
            back_send.at[layer, turn],
            back_recv.at[z, turn],
            at(layer, x),
        )

    def half_rows(column, part):
        return pl.ds(pl.multiple_of(column * rows + part * half, half), half)

    def two_terms(values):
        high = values.astype(jnp.bfloat16)
        return high, (values - high.astype(jnp.float32)).astype(jnp.bfloat16)

    def four_products(stacked, high, low, contract):
        count = stacked.shape[0] // 2
        dot = functools.partial(
            lax.dot_general,
            dimension_numbers=(contract, ((), ())),
            preferred_element_type=jnp.float32,
        )
        by_high, by_low = dot(stacked, high), dot(stacked, low)
        return by_high[:count] + (by_high[count:] + by_low[:count] + by_low[count:])

    def prepare_rows(column, part):
        where = half_rows(column, part)
        values = layer_points[where, :]
        total = jnp.sum(values * values, axis=1, keepdims=True)
        layer_sq[column * 2 + part] = jnp.broadcast_to(total, (half, 128)).T[0:1, :]
        points_high[where, :], points_low[where, :] = two_terms(values)
        probes_high[where, :], probes_low[where, :] = two_terms(layer_probes[where, :])

    def prepare_visitor(layer, begin=0, count=piece):
        values = visitors[layer, begin : begin + count, :]
        visitor_sq[layer, begin : begin + count] = jnp.sum(values * values, axis=1, keepdims=True)
        high, low = two_terms(values)
        visitor_terms[layer, begin : begin + count, :] = high
        visitor_terms[layer, piece + begin : piece + begin + count, :] = low

    def pair(layer, column, parts, fresh=False, begin=0, count=piece):
        first = parts[0]
        where = pl.ds(pl.multiple_of(column * rows + first * half, half), half * len(parts))
        cross = four_products(
            jnp.concatenate(
                [
                    visitor_terms[layer, begin : begin + count, :],
                    visitor_terms[layer, piece + begin : piece + begin + count, :],
                ],
                axis=0,
            ),
            points_high[where, :],
            points_low[where, :],
            ((1,), (1,)),
        )
        row_sq = jnp.concatenate([layer_sq[column * 2 + part] for part in parts], axis=1)
        arg = (visitor_sq[layer, begin : begin + count] + row_sq - 2.0 * cross) * scale
        value = jnp.exp(-jnp.maximum(arg, 0.0))
        product = four_products(
            jnp.concatenate(two_terms(value), axis=0),
            probes_high[where, :],
            probes_low[where, :],
            ((1,), (0,)),
        )
        kept = slice(begin, begin + count)
        sums[layer, kept, :] = product if fresh else sums[layer, kept, :] + product

    barrier = pltpu.get_barrier_semaphore()
    for step in range(1, outer):
        pl.semaphore_signal(barrier, inc=1, device_id=at(lax.rem(z + step, outer), x), device_id_type=MESH)
    for step in range(1, inner):
        pl.semaphore_signal(barrier, inc=1, device_id=at(z, lax.rem(x + step, inner)), device_id_type=MESH)
    pl.semaphore_signal(barrier, inc=1, device_id=sibling, device_id_type=MESH)
    mine = pl.ds(pl.multiple_of(x * rows, rows), rows)
    loads = [
        pltpu.make_async_copy(points_hbm, layer_points.at[mine], load_sem.at[0]),
        pltpu.make_async_copy(probes_hbm, layer_probes.at[mine], load_sem.at[1]),
        pltpu.make_async_copy(points_hbm.at[own_rows], visitors.at[z], load_sem.at[2]),
    ]
    for load in loads:
        load.start()
    pl.semaphore_wait(barrier, outer - 1 + inner - 1 + 1)

    for way in (1, -1):
        @pl.when(inside(z + way))
        def _(way=way):
            onward(z, way, 0, first=True).start()
            onward(z, way, 1, first=True).start()
    for part in range(2):
        for step in range(1, inner):
            for copy in across(step, part):
                copy.start()

    for load in loads:
        load.wait()
    prepare_rows(x, 0)
    prepare_rows(x, 1)
    prepare_visitor(z)
    pair(z, x, (0, 1), fresh=True)

    def both_ways(distance, work):
        def one(k, carry):
            layer = z + (1 - 2 * k) * distance

            @pl.when(inside(layer))
            def _():
                work(layer, 1 - 2 * k)
            return carry
        lax.fori_loop(0, 2, one, 0)

    def receive(distance, turn):
        def work(layer, way):
            wait_recv(visitors.at[layer, pl.ds(turn * (piece // 2), piece // 2)], visit_recv.at[layer, turn])

            @pl.when(inside(z - way))
            def _():
                onward(layer, -way, turn).start()
        both_ways(distance, work)

    def others(work):
        def one(step, carry):
            work(step, lax.rem(x + step, inner))
            return carry
        lax.fori_loop(1, inner, one, 0)

    def take_rows(part):
        def take(step, column):
            wait_rows(column, part, core)
            for copy in share(step, part):
                copy.start()
        others(take)

    def use_rows(part, reach):
        def use(step, column):
            wait_rows(column, part, 1 - core)
            prepare_rows(column, part)

            def one(k, carry):
                layer = z + k - reach

                @pl.when(inside(layer))
                def _():
                    pair(layer, column, (part,))
                    if part == 1:
                        @pl.when((layer != z) & (step == inner - 1))
                        def _():
                            back(layer, 0).start()
                            back(layer, 1).start()
                return carry
            lax.fori_loop(0, 2 * reach + 1, one, 0)
        others(use)

    def meet_own(layer, way):
        prepare_visitor(layer)
        pair(layer, x, (0, 1), fresh=True)

    near = min(2, outer - 1)
    receive(1, 0)
    receive(1, 1)
    both_ways(1, meet_own)
    take_rows(0)
    if near == 2:
        receive(2, 0)
    use_rows(0, 1)
    if near == 2:
        receive(2, 1)

        def meet_more(layer, way):
            meet_own(layer, way)
            others(lambda step, column: pair(layer, column, (0,)))
        both_ways(2, meet_more)
    take_rows(1)
    use_rows(1, near)

    def meet_all(layer, turn):
        here = dict(begin=turn * (piece // 2), count=piece // 2)
        prepare_visitor(layer, **here)
        for column in range(0, inner, 2):
            pair(layer, column, (0, 1, 2, 3), fresh=column == 0, **here)
        back(layer, turn).start()
    for distance in range(near + 1, outer):
        for turn in range(2):
            receive(distance, turn)
            both_ways(distance, lambda layer, way, turn=turn: meet_all(layer, turn))

    for way in (1, -1):
        @pl.when(inside(z + way))
        def _(way=way):
            onward(z, way, 0, first=True).wait_send()
            onward(z, way, 1, first=True).wait_send()

    def sent(layer, way):
        @pl.when(inside(z - way))
        def _():
            onward(layer, -way, 0).wait_send()
            onward(layer, -way, 1).wait_send()
    for distance in range(1, outer):
        both_ways(distance, sent)
    for part in range(2):
        for step in range(1, inner):
            for copy in across(step, part) + share(step, part):
                copy.wait_send()

    result = sums[z]
    for step in range(1, outer):
        layer = lax.rem(z + step, outer)
        for turn in range(2):
            wait_recv(returned.at[layer, pl.ds(turn * (piece // 2), piece // 2)], back_recv.at[layer, turn])
        result = result + returned[layer]
    out_ref[...] = result
    for step in range(1, outer):
        for turn in range(2):
            back(lax.rem(z + step, outer), turn).wait_send()


def body(points, probes):
    rows, width = points.shape
    count = probes.shape[1]
    blocks = lax.axis_size("blk")
    inner = 1 << ((blocks.bit_length() - 1) // 2)
    outer = blocks // inner
    piece = rows // lax.axis_size("team")
    f32, bf16 = jnp.float32, jnp.bfloat16
    dma = pltpu.SemaphoreType.DMA
    return pl.pallas_call(
        functools.partial(kernel, outer, inner),
        out_shape=jax.ShapeDtypeStruct((piece, count), f32),
        in_specs=[pl.BlockSpec(memory_space=pl.ANY)] * 2,
        out_specs=pl.BlockSpec(memory_space=pltpu.VMEM),
        scratch_shapes=[
            pltpu.VMEM((inner * rows, width), f32),
            pltpu.VMEM((inner * rows, count), f32),
            pltpu.VMEM((inner * rows, width), bf16),
            pltpu.VMEM((inner * rows, width), bf16),
            pltpu.VMEM((inner * rows, count), bf16),
            pltpu.VMEM((inner * rows, count), bf16),
            pltpu.VMEM((inner * 2, 1, rows // 2), f32),
            pltpu.VMEM((outer, piece, width), f32),
            pltpu.VMEM((outer, 2 * piece, width), bf16),
            pltpu.VMEM((outer, piece, 1), f32),
            pltpu.VMEM((outer, piece, count), f32),
            pltpu.VMEM((outer, piece, count), f32),
            dma((3,)),
            dma((outer, 2, 2)),
            dma((outer, 2)),
            dma((inner - 1, 2, 2)),
            dma((inner - 1, 2, 2)),
            dma((inner * 4, 2)),
            dma((outer, 2)),
            dma((outer, 2)),
        ],
        compiler_params=pltpu.CompilerParams(collective_id=0, has_side_effects=True),
    )(points, probes)


def solution(mesh):
    in_specs = (P("blk", None), P("blk", None))
    out_specs = P(("blk", "team"), None)
    return jax.shard_map(body, mesh=mesh, in_specs=in_specs, out_specs=out_specs, check_vma=False)
```
